32 devices in a mesh: groups: 2 (over y), section: 2 (over core), row: 2 (over x), col: 4 (over z).
Axes of the slice: x: 2, y: 2, z: 4, core: 2. Of those that a mesh axis runs over, the one named last changes fastest.
Arguments:
- hidden: bfloat16 [2, 2, 3072, 8192], P('section', None, ('groups', 'col'), 'row'), parts along dimension 2, may hold values from -400 to 400
- upstream: bfloat16 [2, 3072, 8192], P(None, ('groups', 'col'), 'row'), parts along dimension 1, may hold values from -8 to 8
- weights: bfloat16 [2, 8192, 8192], P('section', 'row', 'col'), may hold values from -0.0625 to 0.0625
- norm_gains: bfloat16 [2, 8192], P('section', 'row'), may hold values from 0.5 to 1.5
- steering: bfloat16 [16384], P(('groups', 'row')), parts along dimension 0, may hold values from -18 to 18
- steer_layer: int32 [2, 3072], P(None, ('groups', 'col')), parts along dimension 1, may hold values from 0 to 1
Outputs:
- section_grads: bfloat16 [2, 2, 3072, 8192], P('section', None, ('groups', 'col'), 'row'), parts along dimension 2
- steer_grad: float32 [16384], P(('groups', 'row')), parts along dimension 0
The draws below stay inside these ranges and needn't reach their ends.
There are 2 independent parts, one for each index of `groups`. The reference program is written for one: setup_inputs(seed, part) draws one part's arguments, and reference() takes and returns one part's arrays. A program takes and returns all parts, laid end to end along the dimension named above; an argument that names none is the same for every part. Nothing has to cross between parts.
All inputs are finite; a program needn't handle non-finite values.
Results may differ from the reference program's by a relative error of at most 0.0038.
Values may be sent and summed in bfloat16 or wider, within the bound.
A program may use at most 320 MiB of HBM per device.

```python
import math
import jax
import jax.numpy as jnp
from jax import lax

D = 8192
ROWS = 1536
MICRO = 2
SECTIONS = 2


def shared_parts(key):
    key_common, key_column, key_scale = jax.random.split(jax.random.fold_in(key, 101), 3)
    common = jnp.clip(jax.random.normal(key_common, (MICRO, ROWS, D), jnp.float32), -5.0, 5.0)
    row_scale = jnp.exp(jax.random.uniform(key_scale, (MICRO, ROWS, 1), jnp.float32, math.log(0.3), math.log(3.0)))
    column = jnp.exp(jax.random.uniform(key_column, (D,), jnp.float32, 0.0, math.log(10.0)))
    return (common, column, row_scale)


def draw_hidden(key, part):
    common, column, row_scale = shared_parts(key)
    own = jnp.clip(jax.random.normal(jax.random.fold_in(key, 202), (SECTIONS, MICRO, ROWS, D), jnp.float32), -5.0, 5.0)
    values = (common[None] + 0.7 * own) * column * row_scale[None]
    return values.astype(jnp.bfloat16)


def draw_upstream(key, part):
    common, column, row_scale = shared_parts(key)
    noise = jnp.clip(jax.random.normal(jax.random.fold_in(key, 303), (MICRO, ROWS, D), jnp.float32), -5.0, 5.0)
    return (noise + 0.5 * common).astype(jnp.bfloat16)


def set_ends(result, own_key, smallest, largest):
    shape = result.shape
    place = [jax.random.randint(jax.random.fold_in(own_key, axis), (), 0, shape[axis]) for axis in range(len(shape))]
    result = result.at[tuple(place)].set(smallest)
    longest = shape.index(max(shape))
    place[longest] = (place[longest] + 1) % shape[longest]
    return result.at[tuple(place)].set(largest)


def block_levels(own_key, shape, pieces, smallest, largest):
    loudness, own = 1.0, jax.random.fold_in(own_key, 6)
    for dim, shards_of in pieces:
        heights = jnp.exp(jax.random.uniform(jax.random.fold_in(own, dim), (shards_of,), jnp.float32, smallest / len(pieces), largest / len(pieces)))
        loudness = loudness * jnp.repeat(heights, shape[dim] // shards_of).reshape([-1 if axis == dim else 1 for axis in range(len(shape))])
    return loudness


def normal_values(stream_key, dims, width, bound, shards=(), kind=jnp.bfloat16):
    array = jax.random.normal(stream_key, dims, jnp.float32) * width
    if len(shards) > 0:
        array = block_levels(stream_key, dims, shards, -0.22, 0.18) * array
    return jnp.clip(array, min=-bound, max=bound).astype(kind)


def setup_inputs(seed: int = 0, part: int = 0) -> dict:
    arg_keys = jax.random.split(jax.random.key(seed), 7)
    part_keys = jax.random.split(jax.random.fold_in(arg_keys[6], part), 7)
    return {
        "hidden": draw_hidden(jax.random.fold_in(jax.random.fold_in(arg_keys[6], part), 71), part),
        "upstream": draw_upstream(jax.random.fold_in(jax.random.fold_in(arg_keys[6], part), 71), part),
        "weights": normal_values(arg_keys[2], (SECTIONS, D, D), D ** -0.5, 0.0625, ((0, 2), (1, 2), (2, 4))),
        "norm_gains": jnp.clip(1.0 + 0.1 * jax.random.normal(arg_keys[3], (SECTIONS, D), jnp.float32), 0.5, 1.5).astype(jnp.bfloat16),
        "steering": normal_values(part_keys[4], (D,), 3.0, 18.0, ((0, 2),)),
        "steer_layer": set_ends(jax.random.randint(part_keys[5], (MICRO, ROWS), 0, SECTIONS), jax.random.fold_in(part_keys[5], 1), 0, SECTIONS - 1).astype(jnp.int32),
    }


epsilon = 1e-06

def reference(hidden, upstream, weights, norm_gains, steering, steer_layer):
    steer_vec = steering.astype(jnp.float32)
    incoming = [upstream[micro_index] for micro_index in range(MICRO)]
    section_blocks = [None] * SECTIONS
    steer_sum = jnp.zeros((D,), jnp.float32)
    for section_index in reversed(range(SECTIONS)):
        scaling = norm_gains[section_index].astype(jnp.float32)
        passed_list = []
        for micro_index in range(MICRO):
            steered = (steer_layer[micro_index] == section_index)[:, None]
            unsteered = hidden[section_index, micro_index].astype(jnp.float32)
            moved = unsteered + steer_vec
            norm_plain = jnp.sqrt(lax.optimization_barrier(jnp.sum(unsteered * unsteered, -1, keepdims=True)) + epsilon)
            norm_moved = jnp.sqrt(lax.optimization_barrier(jnp.sum(moved * moved, -1, keepdims=True)) + epsilon)
            rescale = norm_plain / norm_moved
            rescaled = jnp.where(steered, moved * rescale, unsteered)
            root_mean = jnp.sqrt(lax.optimization_barrier(jnp.mean(rescaled * rescaled, -1, keepdims=True)) + epsilon)
            grad_float = incoming[micro_index].astype(jnp.float32)
            normal_grad = jnp.dot(incoming[micro_index], weights[section_index].T, preferred_element_type=jnp.float32)
            scaled = scaling * normal_grad
            curvature = lax.optimization_barrier(jnp.sum(scaled * rescaled, -1, keepdims=True))
            input_grad = grad_float + scaled / root_mean - rescaled * curvature / (D * root_mean ** 3)
            direction = moved / norm_moved
            radial = lax.optimization_barrier(jnp.sum(direction * input_grad, -1, keepdims=True))
            tangent = rescale * (input_grad - direction * radial)
            below = jnp.where(steered, tangent + unsteered / norm_plain * radial, input_grad)
            steer_sum = steer_sum + lax.optimization_barrier(jnp.sum(jnp.where(steered, tangent, 0.0), 0))
            passed_list.append(below.astype(jnp.bfloat16))
        incoming = passed_list
        section_blocks[section_index] = jnp.stack(passed_list)
    return (jnp.stack(section_blocks), steer_sum / (MICRO * ROWS))
```

```python
import jax
import jax.numpy as jnp
from jax import lax
from jax.sharding import PartitionSpec as P

D = 8192
ROWS = 1536
MICRO = 2


epsilon = 1e-06


def passed_along(value, axis, steps):
    count = lax.axis_size(axis)
    initial, last = (max(0, -steps), min(count, count - steps))
    return lax.ppermute(value, axis, [(source, source + steps) for source in range(initial, last)])


def local(hidden, upstream, weights, norm_gains, steering, steer_layer):
    sections = lax.axis_size("section")
    section_index = lax.axis_index("section")
    scaling = norm_gains[0].astype(jnp.float32)
    steer_vec = steering.astype(jnp.float32)
    unsteered_all = hidden[0].astype(jnp.float32)
    moved_all = unsteered_all + steer_vec
    row_count = unsteered_all.shape[1]
    feature_count = unsteered_all.shape[2]
    local_weight = weights[0]
    contract = (((1,), (1,)), ((), ()))

    def regroup(full):
        split = full.reshape(row_count, cols, groups, piece)
        return jnp.swapaxes(split, 1, 2).reshape(row_count, cols * groups * piece)

    groups = lax.axis_size("groups")
    cols = lax.axis_size("col")
    piece = local_weight.shape[1] // groups
    own_piece = lax.dynamic_slice_in_dim(local_weight, lax.axis_index("groups") * piece, piece, 1)
    full_weight = lax.all_gather(own_piece, ("groups", "col"), axis=1, tiled=True)
    ticks = MICRO + sections - 1
    received = jnp.zeros((row_count, feature_count), jnp.bfloat16)
    results = jnp.zeros((MICRO, row_count, feature_count), jnp.bfloat16)
    steer_part = jnp.zeros((feature_count,), jnp.float32)
    slots = jnp.arange(MICRO, dtype=jnp.int32)
    for tick_index in range(ticks):
        micro_index = tick_index - (sections - 1 - section_index)
        active = (micro_index >= 0) & (micro_index < MICRO)
        clipped = jnp.clip(micro_index, 0, MICRO - 1)
        if tick_index < MICRO:
            upstream_block = upstream[tick_index]
        else:
            upstream_block = jnp.zeros_like(upstream[0])
        grad_in = jnp.where(section_index == sections - 1, upstream_block, received)
        unsteered = lax.dynamic_index_in_dim(unsteered_all, clipped, 0, keepdims=False)
        moved = lax.dynamic_index_in_dim(moved_all, clipped, 0, keepdims=False)
        layer_rows = lax.dynamic_index_in_dim(steer_layer, clipped, 0, keepdims=False)
        steered = layer_rows == section_index
        steered_col = steered[:, None]
        normal_grad = lax.dot_general(
            regroup(lax.all_gather(grad_in, "row", axis=1, tiled=True)),
            full_weight,
            contract,
            preferred_element_type=jnp.float32,
        )
        grad_float = grad_in.astype(jnp.float32)
        scaled = scaling * normal_grad
        plain_local = jnp.sum(unsteered * unsteered, -1)
        moved_local = jnp.sum(moved * moved, -1)
        scaled_plain = jnp.sum(scaled * unsteered, -1)
        scaled_moved = jnp.sum(scaled * moved, -1)
        plain_sq, moved_sq, curve_plain, curve_moved = lax.psum(
            (plain_local, moved_local, scaled_plain, scaled_moved), "row"
        )
        norm_plain = jnp.sqrt(plain_sq + epsilon)
        norm_moved = jnp.sqrt(moved_sq + epsilon)
        rescale = norm_plain / norm_moved
        square_sum = jnp.where(
            steered, norm_plain * norm_plain * moved_sq / (norm_moved * norm_moved), plain_sq
        )
        root_mean = jnp.sqrt(square_sum / D + epsilon)
        curvature = jnp.where(steered, rescale * curve_moved, curve_plain)
        rescaled = jnp.where(steered_col, moved * rescale[:, None], unsteered)
        factor = curvature / (D * root_mean**3)
        input_grad = grad_float + scaled / root_mean[:, None] - rescaled * factor[:, None]
        direction = moved / norm_moved[:, None]
        radial = lax.psum(jnp.sum(direction * input_grad, -1), "row")
        tangent = rescale[:, None] * (input_grad - direction * radial[:, None])
        below = jnp.where(
            steered_col, tangent + unsteered / norm_plain[:, None] * radial[:, None], input_grad
        )
        passed = jnp.where(active, below, 0.0).astype(jnp.bfloat16)
        results = jnp.where((slots == micro_index)[:, None, None], passed[None], results)
        steer_part = steer_part + jnp.sum(jnp.where(active & steered_col, tangent, 0.0), 0)
        if tick_index + 1 < ticks:
            received = passed_along(passed, "section", -1)
    steer_total = lax.psum(steer_part, ("section", "col"))
    return (results[None], steer_total / (MICRO * ROWS))


def solution(mesh):
    placed = (
        P("section", None, ("groups", "col"), "row"),
        P(None, ("groups", "col"), "row"),
        P("section", "row", "col"),
        P("section", "row"),
        P(("groups", "row")),
        P(None, ("groups", "col")),
    )
    return jax.shard_map(
        local,
        mesh=mesh,
        in_specs=placed,
        out_specs=(P("section", None, ("groups", "col"), "row"), P(("groups", "row"))),
        check_vma=False,
    )
```

```python
import jax
import jax.numpy as jnp
from jax import lax
from jax.sharding import PartitionSpec as P

D = 8192
ROWS = 1536
MICRO = 2


epsilon = 1e-06


def shifted(value, axis, steps=1):
    count = lax.axis_size(axis)
    return lax.ppermute(value, axis, [(source, (source + steps) % count) for source in range(count)])


def columns(value, start, width):
    return lax.dynamic_slice_in_dim(value, start, width, value.ndim - 1)


def after(value, earlier):
    return lax.optimization_barrier((value, earlier))[0]


def local(hidden, upstream, weights, norm_gains, steering, steer_layer):
    core = lax.axis_index("section")
    row_index = lax.axis_index("row")
    col_index = lax.axis_index("col")
    group = lax.axis_index("groups")
    row_devices = lax.axis_size("row")
    cols = lax.axis_size("col")
    groups = lax.axis_size("groups")
    micro, row_count, features = upstream.shape
    tokens = micro * row_count
    half = features // 2
    depth = weights.shape[2]
    part = depth // groups
    f32 = jnp.float32

    def own_columns(value):
        return columns(value, core * half, half)

    def per_section(mine, received):
        return jnp.where(core == 0, mine, received), jnp.where(core == 1, mine, received)

    def over_cores(value, axis):
        mine = lax.dynamic_slice_in_dim(value, core * half, half, axis)
        given = lax.dynamic_slice_in_dim(value, (1 - core) * half, half, axis)
        return per_section(mine, shifted(given, "section"))

    weight_of = over_cores(weights[0], 0)
    hidden_of = over_cores(hidden[0].reshape(tokens, features), 1)
    gain_of = over_cores(norm_gains[0], 0)
    steer_vec = own_columns(steering).astype(f32)
    layers = steer_layer.reshape(tokens)
    upstream_rows = upstream.reshape(tokens, features)

    earlier, sent = [], []
    pieces = {}
    for section, count in ((1, 2), (0, 4)):
        count = max(1, min(count, part // 128))
        width = part // count
        held = []
        for chunk in range(count):
            own = columns(weight_of[section], group * part + chunk * width, width)
            own = after(own, tuple(earlier))
            gathered = lax.all_gather(own, "col", axis=1, tiled=True)
            others = jnp.concatenate(
                [columns(gathered, ((col_index + step) % cols) * width, width) for step in range(1, cols)], 1
            )
            held.append((others, shifted(others, "groups")))
            earlier = [others] + [held_before[1] for held_before in sent[-1:]]
            sent.append(held[-1])
        pieces[section] = (width, held)

    def projected(full, section):
        width, held = pieces[section]

        def times(left, right):
            return lax.dot_general(left, right, (((1,), (1,)), ((), ())), preferred_element_type=f32)

        total = times(columns(full, col_index * depth, depth), weight_of[section])
        for chunk, sides in enumerate(held):
            for side, block in enumerate(sides):
                owner = (group + side) % groups
                start = owner * part + chunk * width
                left = jnp.concatenate(
                    [columns(full, ((col_index + step) % cols) * depth + start, width) for step in range(1, cols)], 1
                )
                total = total + times(left, block)
        return total

    def all_features(own):
        if row_devices == 2:
            other = shifted(own, "row")
            both = jnp.concatenate([jnp.where(row_index == 0, own, other), jnp.where(row_index == 0, other, own)], 1)
            if own.shape[1] == features:
                return both
            there = shifted(both, "section")
            lower = jnp.where(core == 0, both, there)
            upper = jnp.where(core == 0, there, both)
            return jnp.concatenate([lower[:, :half], upper[:, :half], lower[:, half:], upper[:, half:]], 1)
        if own.shape[1] == features:
            return lax.all_gather(own, "row", axis=1, tiled=True)
        return lax.all_gather(own, ("row", "section"), axis=1, tiled=True)

    local_sums = []
    for section in range(2):
        unsteered = hidden_of[section].astype(f32)
        moved = unsteered + steer_vec
        local_sums += [jnp.sum(unsteered * unsteered, -1), jnp.sum(moved * moved, -1)]
    sums = lax.psum(tuple(local_sums), ("row", "section"))

    incoming = own_columns(upstream_rows)
    full = all_features(upstream_rows)
    steer_part = jnp.zeros((half,), f32)
    blocks = [None, None]
    for section in (1, 0):
        plain_sq, moved_sq = sums[2 * section], sums[2 * section + 1]
        steered = layers == section
        steered_col = steered[:, None]
        unsteered = hidden_of[section].astype(f32)
        moved = unsteered + steer_vec
        grad_float = incoming.astype(f32)
        scaled = gain_of[section].astype(f32) * projected(full, section)
        chosen = jnp.where(steered_col, moved, unsteered)
        curve, inner = lax.psum(
            (jnp.sum(scaled * chosen, -1), jnp.sum(grad_float * moved, -1)), ("row", "section")
        )
        norm_plain = jnp.sqrt(plain_sq + epsilon)
        norm_moved = jnp.sqrt(moved_sq + epsilon)
        rescale = norm_plain / norm_moved
        square_sum = jnp.where(
            steered, norm_plain * norm_plain * moved_sq / (norm_moved * norm_moved), plain_sq
        )
        root_mean = jnp.sqrt(square_sum / D + epsilon)
        scale = jnp.where(steered, rescale, 1.0)
        factor = scale * curve / (D * root_mean**3)
        input_grad = grad_float + scaled / root_mean[:, None] - chosen * (scale * factor)[:, None]
        radial = (inner + curve / root_mean - rescale * factor * moved_sq) / norm_moved
        tangent = rescale[:, None] * (input_grad - moved * (radial / norm_moved)[:, None])
        below = jnp.where(steered_col, tangent + unsteered * (radial / norm_plain)[:, None], input_grad)
        passed = below.astype(jnp.bfloat16)
        blocks[section] = passed
        steer_part = steer_part + jnp.sum(jnp.where(steered_col, tangent, 0.0), 0)
        if section == 1:
            incoming = passed
            full = all_features(passed)
    kept = jnp.where(core == 0, blocks[0], blocks[1])
    received = shifted(jnp.where(core == 0, blocks[1], blocks[0]), "section")
    lower = jnp.where(core == 0, kept, received)
    upper = jnp.where(core == 0, received, kept)
    result = jnp.concatenate([lower, upper], 1).reshape(1, micro, row_count, features)
    slots = jnp.where(jnp.arange(2)[:, None] == core, steer_part[None], 0.0).reshape(features)
    steer_total = lax.psum(slots, ("section", "col"))
    return (result, steer_total / (MICRO * ROWS))


def solution(mesh):
    placed = (
        P("section", None, ("groups", "col"), "row"),
        P(None, ("groups", "col"), "row"),
        P("section", "row", "col"),
        P("section", "row"),
        P(("groups", "row")),
        P(None, ("groups", "col")),
    )
    return jax.shard_map(
        local,
        mesh=mesh,
        in_specs=placed,
        out_specs=(P("section", None, ("groups", "col"), "row"), P(("groups", "row"))),
        check_vma=False,
    )
```

```python
import jax
import jax.numpy as jnp
from jax import lax
from jax.sharding import PartitionSpec as P

D = 8192
ROWS = 1536
MICRO = 2


epsilon = 1e-06


def shifted(value, axis, steps=1):
    count = lax.axis_size(axis)
    return lax.ppermute(value, axis, [(source, (source + steps) % count) for source in range(count)])


def columns(value, start, width):
    return lax.dynamic_slice_in_dim(value, start, width, value.ndim - 1)


def after(value, earlier):
    return lax.optimization_barrier((value, earlier))[0]


def local(hidden, upstream, weights, norm_gains, steering, steer_layer):
    core = lax.axis_index("section")
    row_index = lax.axis_index("row")
    col_index = lax.axis_index("col")
    group = lax.axis_index("groups")
    row_devices = lax.axis_size("row")
    cols = lax.axis_size("col")
    groups = lax.axis_size("groups")
    micro, row_count, features = upstream.shape
    tokens = micro * row_count
    half = features // 2
    depth = weights.shape[2]
    part = depth // groups
    f32 = jnp.float32

    def own_columns(value):
        return columns(value, core * half, half)

    def per_section(mine, received):
        return jnp.where(core == 0, mine, received), jnp.where(core == 1, mine, received)

    def over_cores(value, axis):
        mine = lax.dynamic_slice_in_dim(value, core * half, half, axis)
        given = lax.dynamic_slice_in_dim(value, (1 - core) * half, half, axis)
        return per_section(mine, shifted(given, "section"))

    units = max(1, part // 128)
    step_units = max(1, units // 4)
    unit = part // units
    widths_of = {}
    for section in (1, 0):
        sizes = [step_units] * (units // step_units)
        if sum(sizes) < units:
            sizes.append(units - sum(sizes))
        widths_of[section] = [size * unit for size in sizes]
    mine = lax.dynamic_slice_in_dim(weights[0], core * half, half, 0)
    given = lax.dynamic_slice_in_dim(weights[0], (1 - core) * half, half, 0)
    lead = widths_of[1][0]
    lead_given = shifted(columns(given, group * part, lead), "section")
    first_pieces = per_section(columns(mine, group * part, lead), lead_given)
    weight_of = per_section(mine, shifted(after(given, lead_given), "section"))
    hidden_of = over_cores(hidden[0].reshape(tokens, features), 1)
    gain_of = over_cores(norm_gains[0], 0)
    steer_vec = own_columns(steering).astype(f32)
    layers = steer_layer.reshape(tokens)
    upstream_rows = upstream.reshape(tokens, features)

    earlier, sent = [], []
    pieces = {}
    for section in (1, 0):
        held = []
        start = 0
        for width in widths_of[section]:
            own = first_pieces[section] if start == 0 else columns(weight_of[section], group * part + start, width)
            if earlier:
                own = after(own, tuple(earlier))
            gathered = lax.all_gather(own, "col", axis=1, tiled=True)
            others = jnp.concatenate(
                [columns(gathered, ((col_index + step) % cols) * width, width) for step in range(1, cols)], 1
            )
            held.append((start, width, (others, shifted(others, "groups"))))
            earlier = [others] + sent[-1:]
            sent.append(held[-1][2][1])
            start += width
        pieces[section] = held

    def projected(full, section):
        def times(left, right):
            return lax.dot_general(left, right, (((1,), (1,)), ((), ())), preferred_element_type=f32)

        total = times(columns(full, col_index * depth, depth), weight_of[section])
        held = pieces[section]
        for start, width, sides in held:
            total = lax.optimization_barrier(total)
            for side, block in enumerate(sides):
                offset = ((group + side) % groups) * part + start
                left = jnp.concatenate(
                    [columns(full, ((col_index + step) % cols) * depth + offset, width) for step in range(1, cols)], 1
                )
                total = total + times(left, block)
        return total

    def all_features(own):
        if row_devices == 2:
            other = shifted(own, "row")
            both = jnp.concatenate([jnp.where(row_index == 0, own, other), jnp.where(row_index == 0, other, own)], 1)
            if own.shape[1] == features:
                return both
            there = shifted(both, "section")
            lower = jnp.where(core == 0, both, there)
            upper = jnp.where(core == 0, there, both)
            return jnp.concatenate([lower[:, :half], upper[:, :half], lower[:, half:], upper[:, half:]], 1)
        if own.shape[1] == features:
            return lax.all_gather(own, "row", axis=1, tiled=True)
        return lax.all_gather(own, ("row", "section"), axis=1, tiled=True)

    local_sums = []
    for section in range(2):
        unsteered = hidden_of[section].astype(f32)
        moved = unsteered + steer_vec
        local_sums += [jnp.sum(unsteered * unsteered, -1), jnp.sum(moved * moved, -1)]
    sums = lax.psum(tuple(local_sums), ("row", "section"))

    incoming = own_columns(upstream_rows)
    full = all_features(upstream_rows)
    steer_part = jnp.zeros((half,), f32)
    blocks = [None, None]
    for section in (1, 0):
        plain_sq, moved_sq = sums[2 * section], sums[2 * section + 1]
        steered = layers == section
        steered_col = steered[:, None]
        unsteered = hidden_of[section].astype(f32)
        moved = unsteered + steer_vec
        grad_float = incoming.astype(f32)
        scaled = gain_of[section].astype(f32) * projected(full, section)
        chosen = jnp.where(steered_col, moved, unsteered)
        curve, inner = lax.psum(
            (jnp.sum(scaled * chosen, -1), jnp.sum(grad_float * moved, -1)), ("row", "section")
        )
        norm_plain = jnp.sqrt(plain_sq + epsilon)
        norm_moved = jnp.sqrt(moved_sq + epsilon)
        rescale = norm_plain / norm_moved
        square_sum = jnp.where(
            steered, norm_plain * norm_plain * moved_sq / (norm_moved * norm_moved), plain_sq
        )
        root_mean = jnp.sqrt(square_sum / D + epsilon)
        scale = jnp.where(steered, rescale, 1.0)
        factor = scale * curve / (D * root_mean**3)
        input_grad = grad_float + scaled / root_mean[:, None] - chosen * (scale * factor)[:, None]
        radial = (inner + curve / root_mean - rescale * factor * moved_sq) / norm_moved
        tangent = rescale[:, None] * (input_grad - moved * (radial / norm_moved)[:, None])
        below = jnp.where(steered_col, tangent + unsteered * (radial / norm_plain)[:, None], input_grad)
        passed = below.astype(jnp.bfloat16)
        blocks[section] = passed
        steer_part = steer_part + jnp.sum(jnp.where(steered_col, tangent, 0.0), 0)
        if section == 1:
            incoming = passed
            full = all_features(passed)
    kept = jnp.where(core == 0, blocks[0], blocks[1])
    received = shifted(jnp.where(core == 0, blocks[1], blocks[0]), "section")
    lower = jnp.where(core == 0, kept, received)
    upper = jnp.where(core == 0, received, kept)
    result = jnp.concatenate([lower, upper], 1).reshape(1, micro, row_count, features)
    slots = jnp.where(jnp.arange(2)[:, None] == core, steer_part[None], 0.0).reshape(features)
    steer_total = lax.psum(slots, ("section", "col"))
    return (result, steer_total / (MICRO * ROWS))


def solution(mesh):
    placed = (
        P("section", None, ("groups", "col"), "row"),
        P(None, ("groups", "col"), "row"),
        P("section", "row", "col"),
        P("section", "row"),
        P(("groups", "row")),
        P(None, ("groups", "col")),
    )
    return jax.shard_map(
        local,
        mesh=mesh,
        in_specs=placed,
        out_specs=(P("section", None, ("groups", "col"), "row"), P(("groups", "row"))),
        check_vma=False,
    )
```

```python
import jax
import jax.numpy as jnp
from jax import lax
from jax.sharding import PartitionSpec as P

D = 8192
ROWS = 1536
MICRO = 2


epsilon = 1e-06


def shifted(value, axis, steps=1):
    count = lax.axis_size(axis)
    return lax.ppermute(value, axis, [(source, (source + steps) % count) for source in range(count)])


def columns(value, start, width):
    return lax.dynamic_slice_in_dim(value, start, width, value.ndim - 1)


def after(value, earlier):
    return lax.optimization_barrier((value, earlier))[0]


def local(hidden, upstream, weights, norm_gains, steering, steer_layer):
    core = lax.axis_index("section")
    row_index = lax.axis_index("row")
    col_index = lax.axis_index("col")
    group = lax.axis_index("groups")
    row_devices = lax.axis_size("row")
    cols = lax.axis_size("col")
    groups = lax.axis_size("groups")
    micro, row_count, features = upstream.shape
    tokens = micro * row_count
    half = features // 2
    depth = weights.shape[2]
    part = depth // groups
    f32 = jnp.float32

    def own_columns(value):
        return columns(value, core * half, half)

    def per_section(mine, received):
        return jnp.where(core == 0, mine, received), jnp.where(core == 1, mine, received)

    def over_cores(value, axis):
        mine = lax.dynamic_slice_in_dim(value, core * half, half, axis)
        given = lax.dynamic_slice_in_dim(value, (1 - core) * half, half, axis)
        return per_section(mine, shifted(given, "section"))

    units = max(1, part // 128)
    step_units = max(1, units // 4)
    unit = part // units
    widths_of = {}
    for section in (1, 0):
        sizes = [step_units] * (units // step_units)
        if sum(sizes) < units:
            sizes.append(units - sum(sizes))
        widths_of[section] = [size * unit for size in sizes]
    mine = lax.dynamic_slice_in_dim(weights[0], core * half, half, 0)
    given = lax.dynamic_slice_in_dim(weights[0], (1 - core) * half, half, 0)
    lead = sum(widths_of[1][:2])
    lead_given = shifted(columns(given, group * part, lead), "section")
    first_pieces = per_section(columns(mine, group * part, lead), lead_given)
    weight_of = per_section(mine, shifted(after(given, lead_given), "section"))
    hidden_of = over_cores(hidden[0].reshape(tokens, features), 1)
    gain_of = over_cores(norm_gains[0], 0)
    steer_vec = own_columns(steering).astype(f32)
    layers = steer_layer.reshape(tokens)
    upstream_rows = upstream.reshape(tokens, features)

    earlier, sent = [], []
    pieces = {}
    for section in (1, 0):
        held = []
        start = 0
        for width in widths_of[section]:
            if start + width <= lead:
                own = first_pieces[section][:, start : start + width]
            else:
                own = columns(weight_of[section], group * part + start, width)
            if earlier:
                own = after(own, tuple(earlier))
            gathered = lax.all_gather(own, "col", axis=1, tiled=True)
            others = jnp.concatenate(
                [columns(gathered, ((col_index + step) % cols) * width, width) for step in range(1, cols)], 1
            )
            held.append((start, width, (others, shifted(others, "groups"))))
            earlier = [others] + sent[-1:]
            sent.append(held[-1][2][1])
            start += width
        pieces[section] = held

    def projected(full, section):
        def times(left, right):
            return lax.dot_general(left, right, (((1,), (1,)), ((), ())), preferred_element_type=f32)

        total = times(columns(full, col_index * depth, depth), weight_of[section])
        held = pieces[section]
        for start, width, sides in held:
            total = lax.optimization_barrier(total)
            for side, block in enumerate(sides):
                offset = ((group + side) % groups) * part + start
                left = jnp.concatenate(
                    [columns(full, ((col_index + step) % cols) * depth + offset, width) for step in range(1, cols)], 1
                )
                total = total + times(left, block)
        return total

    def all_features(own):
        if row_devices == 2:
            other = shifted(own, "row")
            both = jnp.concatenate([jnp.where(row_index == 0, own, other), jnp.where(row_index == 0, other, own)], 1)
            if own.shape[1] == features:
                return both
            there = shifted(both, "section")
            lower = jnp.where(core == 0, both, there)
            upper = jnp.where(core == 0, there, both)
            return jnp.concatenate([lower[:, :half], upper[:, :half], lower[:, half:], upper[:, half:]], 1)
        if own.shape[1] == features:
            return lax.all_gather(own, "row", axis=1, tiled=True)
        return lax.all_gather(own, ("row", "section"), axis=1, tiled=True)

    local_sums = []
    for section in range(2):
        unsteered = hidden_of[section].astype(f32)
        moved = unsteered + steer_vec
        local_sums += [jnp.sum(unsteered * unsteered, -1), jnp.sum(moved * moved, -1)]
    sums = lax.psum(tuple(local_sums), ("row", "section"))

    incoming = own_columns(upstream_rows)
    full = all_features(upstream_rows)
    steer_part = jnp.zeros((half,), f32)
    blocks = [None, None]
    for section in (1, 0):
        plain_sq, moved_sq = sums[2 * section], sums[2 * section + 1]
        steered = layers == section
        steered_col = steered[:, None]
        unsteered = hidden_of[section].astype(f32)
        moved = unsteered + steer_vec
        grad_float = incoming.astype(f32)
        scaled = gain_of[section].astype(f32) * projected(full, section)
        chosen = jnp.where(steered_col, moved, unsteered)
        curve, inner = lax.psum(
            (jnp.sum(scaled * chosen, -1), jnp.sum(grad_float * moved, -1)), ("row", "section")
        )
        norm_plain = jnp.sqrt(plain_sq + epsilon)
        norm_moved = jnp.sqrt(moved_sq + epsilon)
        rescale = norm_plain / norm_moved
        square_sum = jnp.where(
            steered, norm_plain * norm_plain * moved_sq / (norm_moved * norm_moved), plain_sq
        )
        root_mean = jnp.sqrt(square_sum / D + epsilon)
        scale = jnp.where(steered, rescale, 1.0)
        factor = scale * curve / (D * root_mean**3)
        input_grad = grad_float + scaled / root_mean[:, None] - chosen * (scale * factor)[:, None]
        radial = (inner + curve / root_mean - rescale * factor * moved_sq) / norm_moved
        tangent = rescale[:, None] * (input_grad - moved * (radial / norm_moved)[:, None])
        below = jnp.where(steered_col, tangent + unsteered * (radial / norm_plain)[:, None], input_grad)
        passed = below.astype(jnp.bfloat16)
        blocks[section] = passed
        steer_part = steer_part + jnp.sum(jnp.where(steered_col, tangent, 0.0), 0)
        if section == 1:
            incoming = passed
            full = all_features(passed)
    kept = jnp.where(core == 0, blocks[0], blocks[1])
    received = shifted(jnp.where(core == 0, blocks[1], blocks[0]), "section")
    lower = jnp.where(core == 0, kept, received)
    upper = jnp.where(core == 0, received, kept)
    result = jnp.concatenate([lower, upper], 1).reshape(1, micro, row_count, features)
    steer_own = lax.psum(steer_part, "col")
    steer_other = shifted(steer_own, "section")
    steer_total = jnp.concatenate(
        [jnp.where(core == 0, steer_own, steer_other), jnp.where(core == 0, steer_other, steer_own)]
    )
    return (result, steer_total / (MICRO * ROWS))


def solution(mesh):
    placed = (
        P("section", None, ("groups", "col"), "row"),
        P(None, ("groups", "col"), "row"),
        P("section", "row", "col"),
        P("section", "row"),
        P(("groups", "row")),
        P(None, ("groups", "col")),
    )
    return jax.shard_map(
        local,
        mesh=mesh,
        in_specs=placed,
        out_specs=(P("section", None, ("groups", "col"), "row"), P(("groups", "row"))),
        check_vma=False,
    )
```
